32 devices in a mesh: freq: 4 (over y, x), ma: 8 (over z, core).
Axes of the slice: x: 2, y: 2, z: 4, core: 2. Of those that a mesh axis runs over, the one named last changes fastest.
Arguments:
- sky_coeffs: bfloat16 [4, 2, 3, 256, 8, 16, 128], P('freq', None, None, None, 'ma'), may hold values from -6 to 6
- beam_transfer: bfloat16 [4, 8, 2, 3, 2048, 512], P('freq', 'ma'), may hold values from -0.078125 to 0.078125
- svd_basis: bfloat16 [4, 16, 2, 256, 512], P('freq', 'ma'), may hold values from -0.1875 to 0.1875
- kl_basis: bfloat16 [16, 2, 256, 4, 256], P('ma'), may hold values from -0.1875 to 0.1875
- m_values: int32 [16], P('ma'), may hold values from 1 to 2047, as said below
- svd_count: int32 [16], P('ma'), may hold values from 128 to 256, as said below
- kl_index: int32 [16, 128], P('ma'), may hold values from 0 to 255, as said below
- kl_count: int32 [16], P('ma'), may hold values from 64 to 128, as said below
Outputs:
- kl_modes: bfloat16 [16, 2, 128, 128], P('ma', None, None, 'freq')
The draws below stay inside these ranges and needn't reach their ends.
Inputs may be any that keep to these rules, and one draw needn't show every extreme that they name: `m_values`: for each owner, the sum of 2048 - m over its 2 m-values is at most 2048, and equals 2048 for owner 0. `svd_count`: slot 0 retains all 256 modes. `kl_index`: entries of one m are distinct. `kl_count`: slot 0 retains all 128 modes.
All inputs are finite; a program needn't handle non-finite values.
Results may differ from the reference program's by a relative error of at most 0.012.
Values may be sent and summed in bfloat16 or wider, within the bound.
A program may use at most 128 MiB of HBM per device.

```python
import jax
import jax.numpy as jnp
from jax import lax

L = 2048
BASE = 512
POL = 3
NS = 256
NKL = 256
KEEP = 128
M_DEV = 2
R = 128
NFREQ = 4
OWNERS = 8
LROW = 256
M = 16


def draw_m_values(key, part):
    owner_total = M // M_DEV
    key_first, key_excess = jax.random.split(key)
    first_m = jax.random.randint(key_first, (owner_total,), 1, L)
    excess = jax.random.randint(key_excess, (owner_total,), 0, first_m)
    excess = excess.at[0].set(0)
    second_m = L - first_m + excess
    return jnp.stack([first_m, second_m], 1).reshape(M).astype(jnp.int32)


def draw_svd_count(key, part):
    counts = jax.random.randint(key, (M,), NS // 2, NS + 1)
    return counts.at[0].set(NS).astype(jnp.int32)


def draw_kl_count(key, part):
    counts = jax.random.randint(key, (M,), KEEP // 2, KEEP + 1)
    return counts.at[0].set(KEEP).astype(jnp.int32)


def draw_kl_index(key, part):
    key_list = jax.random.split(key, M)
    chosen = jax.vmap(lambda one_key: jax.random.permutation(one_key, NKL)[:KEEP])(key_list)
    return chosen.astype(jnp.int32)


def steps_of(stream_key, dims, cuts, smallest, largest):
    loudness = 1.0
    for position, blocks in cuts:
        draws = jax.random.uniform(jax.random.fold_in(jax.random.fold_in(stream_key, 6), position), (blocks,), jnp.float32, smallest / len(cuts), largest / len(cuts))
        loudness = loudness * jnp.repeat(jnp.exp(draws), dims[position] // blocks).reshape((-1,) + (1,) * (len(dims) - 1 - position))
    return loudness


def noise(rng, dims, scale, bound, shards=(), held_as=jnp.bfloat16):
    loudness = steps_of(rng, dims, shards, -0.22, 0.18) if shards else 1.0
    entries = jax.random.normal(rng, dims, jnp.float32) * scale * loudness
    return jnp.minimum(jnp.maximum(entries, -bound), bound).astype(held_as)


def setup_inputs(seed: int = 0) -> dict:
    key_of = jax.random.split(jax.random.key(seed), 9)
    sky_coeffs = noise(key_of[0], (NFREQ, 2, POL, LROW, OWNERS, M, R), 1.0, 6.0, ((0, 4), (4, 8)))
    beam_transfer = noise(key_of[1], (NFREQ, OWNERS, 2, POL, L, BASE), (3 * L) ** -0.5, 0.078125, ((0, 4), (1, 8)))
    svd_basis = noise(key_of[2], (NFREQ, M, 2, NS, BASE), (2 * BASE) ** -0.5, 0.1875, ((0, 4), (1, 8)))
    kl_basis = noise(key_of[3], (M, 2, NKL, NFREQ, NS), (NFREQ * NS) ** -0.5, 0.1875, ((0, 8),))
    m_values = draw_m_values(jax.random.fold_in(key_of[8], 71), 0)
    svd_count = draw_svd_count(jax.random.fold_in(key_of[8], 71), 0)
    kl_index = draw_kl_index(jax.random.fold_in(key_of[8], 71), 0)
    kl_count = draw_kl_count(jax.random.fold_in(key_of[8], 71), 0)
    return {"sky_coeffs": sky_coeffs, "beam_transfer": beam_transfer, "svd_basis": svd_basis, "kl_basis": kl_basis, "m_values": m_values, "svd_count": svd_count, "kl_index": kl_index, "kl_count": kl_count}


def pack_rows(sky_freq, m_owner):
    multipoles = sky_freq.shape[2]
    padded = jnp.pad(sky_freq, ((0, 0), (0, 0), (multipoles, multipoles), (0, 0), (0, 0)))
    row_index = jnp.arange(multipoles, dtype=jnp.int32)
    row_start = jnp.zeros((), jnp.int32)
    packed_list = []
    for slot_num in range(sky_freq.shape[3]):
        span_len = (multipoles - m_owner[slot_num]).astype(jnp.int32)
        row_shift = (m_owner[slot_num] - row_start).astype(jnp.int32)
        shifted = lax.dynamic_slice_in_dim(padded[:, :, :, slot_num, :], (multipoles + row_shift).astype(jnp.int32), multipoles, 2)
        row_mask = (row_index >= row_start) & (row_index < row_start + span_len)
        packed_list.append(jnp.where(row_mask[None, None, :, None], shifted, jnp.zeros((), shifted.dtype)))
        row_start = row_start + span_len
    return jnp.stack(packed_list, 3)


def project(sky_freq, beam_owner, svd_owner, m_owner, svd_kept):
    packed = pack_rows(sky_freq, m_owner)
    real_part, imag_part = packed[0], packed[1]
    stacked = jnp.stack([jnp.stack([real_part, -imag_part]), jnp.stack([imag_part, real_part])])
    visibility = jnp.einsum('ocplsr,cplb->osrb', stacked.astype(jnp.float32), beam_owner.astype(jnp.float32)).astype(jnp.bfloat16)
    rotated = jnp.stack([jnp.stack([visibility[0], visibility[1]]), jnp.stack([visibility[1], -visibility[0]])])
    coefficients = jnp.einsum('oqsrb,sqjb->osjr', rotated.astype(jnp.float32), svd_owner.astype(jnp.float32))
    mode_mask = jnp.arange(svd_owner.shape[2], dtype=jnp.int32)[None, :] < svd_kept[:, None]
    return jnp.where(mode_mask[None, :, :, None], coefficients, 0.0).astype(jnp.bfloat16)


def kl_combine(coef_all, selected, kl_kept):
    first_part, second_part = coef_all[0], coef_all[1]
    stacked = jnp.stack([jnp.stack([first_part, -second_part]), jnp.stack([second_part, first_part])])
    kl_out = jnp.einsum('oqsfjr,sqifj->soir', stacked.astype(jnp.float32), selected.astype(jnp.float32))
    mode_mask = jnp.arange(selected.shape[2], dtype=jnp.int32)[None, :] < kl_kept[:, None]
    return jnp.where(mode_mask[:, None, :, None], kl_out, 0.0).astype(jnp.bfloat16)


def reference(sky_coeffs, beam_transfer, svd_basis, kl_basis, m_values, svd_count, kl_index, kl_count):
    sky_full = sky_coeffs.reshape(NFREQ, 2, POL, L, M, R)

    def owner_work(owner_index):
        first_slot = (owner_index * M_DEV).astype(jnp.int32)
        m_owner = lax.dynamic_slice_in_dim(m_values, first_slot, M_DEV, 0)
        svd_kept = lax.dynamic_slice_in_dim(svd_count, first_slot, M_DEV, 0)
        kl_rows = lax.dynamic_slice_in_dim(kl_index, first_slot, M_DEV, 0)
        kl_kept = lax.dynamic_slice_in_dim(kl_count, first_slot, M_DEV, 0)
        coeff_list = []
        for channel in range(NFREQ):
            sky_freq = lax.dynamic_slice_in_dim(sky_full[channel], first_slot, M_DEV, 3)
            beam_owner = lax.dynamic_index_in_dim(beam_transfer[channel], owner_index, 0, keepdims=False)
            svd_owner = lax.dynamic_slice_in_dim(svd_basis[channel], first_slot, M_DEV, 0)
            coeff_list.append(project(sky_freq, beam_owner, svd_owner, m_owner, svd_kept))
        coef_all = jnp.stack(coeff_list, 2)
        basis_owner = lax.dynamic_slice_in_dim(kl_basis, first_slot, M_DEV, 0)
        selected = jax.vmap(lambda basis_one, chosen: jnp.take(basis_one, chosen, axis=1))(basis_owner, kl_rows)
        return kl_combine(coef_all, selected, kl_kept)

    filtered = lax.map(owner_work, jnp.arange(OWNERS, dtype=jnp.int32))
    return filtered.reshape(M, 2, KEEP, R)
```

```python
import functools

import jax
import jax.numpy as jnp
from jax import lax
from jax.experimental import pallas as pl
from jax.experimental.pallas import tpu as pltpu
from jax.sharding import PartitionSpec as P

MESH = pl.DeviceIdType.MESH
F32 = jnp.float32
BF16 = jnp.bfloat16


def partner(me, step, size):
    out, bit = 0, 1
    while bit < size:
        a, b = (me // bit) % 2, (step // bit) % 2
        out = out + bit * (a + b - 2 * a * b)
        bit *= 2
    return out


def exchange_kernel(
    lanes, rows, slots, block, kblock,
    m_ref, sky_ref, beam_ref, vis_ref,
    m_all, m_smem, sky_buf, wide, send, recv, extra_send, extra_recv, beam_buf,
    stage, mixed, turned, acc_r, acc_i,
    m_send, m_recv, m_local, sky_sem, beam_sem, send_sem, recv_sem, ex_send, ex_recv,
):
    me = lax.axis_index("ma")
    chunks = sky_ref.shape[0]
    pols = chunks // 2
    total = lanes * rows
    reals = sky_ref.shape[2]

    for ch in range(chunks):
        pltpu.make_async_copy(sky_ref.at[ch], sky_buf.at[ch], sky_sem.at[ch]).start()
    for part in range(2):
        for pol in range(pols):
            pltpu.make_async_copy(
                beam_ref.at[part, pol], beam_buf.at[part, pol], beam_sem.at[part, pol]
            ).start()

    barrier = pltpu.get_barrier_semaphore()

    @pl.loop(1, lanes)
    def _(step):
        pl.semaphore_signal(
            barrier, inc=1, device_id={"ma": partner(me, step, lanes)}, device_id_type=MESH
        )

    pl.semaphore_wait(barrier, lanes - 1)

    def m_copy(step):
        peer = partner(me, step, lanes)
        return pltpu.make_async_remote_copy(
            src_ref=m_ref, dst_ref=m_all.at[me], send_sem=m_send.at[peer],
            recv_sem=m_recv.at[me], device_id={"ma": peer}, device_id_type=MESH,
        )

    def m_arrival(step):
        peer = partner(me, step, lanes)
        return pltpu.make_async_remote_copy(
            src_ref=m_ref, dst_ref=m_all.at[peer], send_sem=m_send.at[peer],
            recv_sem=m_recv.at[peer], device_id={"ma": peer}, device_id_type=MESH,
        )

    @pl.loop(0, lanes - 1)
    def _(i):
        m_copy(lanes - 1 - i).start()

    m_all[me] = m_ref[...]

    def widen(ch):
        pltpu.make_async_copy(sky_ref.at[ch], sky_buf.at[ch], sky_sem.at[ch]).wait()
        piece = 256

        @pl.loop(0, rows * slots // piece)
        def _(i):
            at = pl.multiple_of(i * piece, piece)
            wide[ch, pl.ds(at, piece), :] = sky_buf[ch, pl.ds(at, piece), :].astype(F32)

        wide[ch, pl.ds(rows * slots, block * slots), :] = jnp.zeros((block * slots, reals), F32)

    widen(0)

    @pl.loop(1, lanes)
    def _(step):
        copy = m_arrival(step)
        copy.wait_recv()
        copy.wait_send()

    local = pltpu.make_async_copy(m_all, m_smem, m_local)
    local.start()
    local.wait()

    row_in_block = lax.broadcasted_iota(jnp.int32, (block, reals), 0)

    def pack(ch):
        @pl.loop(0, lanes)
        def _(owner):
            m0, m1 = m_smem[owner, 0, 0], m_smem[owner, 1, 0]
            start1 = total - m0
            excess = m0 + m1 - total
            first0 = (m0 - me + lanes - 1) // lanes
            first1 = (excess - me + lanes - 1) // lanes
            residue = lanes * first0 + me - m0

            @pl.loop(0, rows // block)
            def _(i):
                k0 = i * block
                r0 = jnp.clip(first0 + k0, 0, rows)
                r1 = jnp.clip(first1 + k0, 0, rows)
                v0 = wide[ch, pl.ds(r0 * slots + 2 * owner, block, stride=slots), :]
                v1 = wide[ch, pl.ds(r1 * slots + 2 * owner + 1, block, stride=slots), :]
                packed_at = lanes * (row_in_block + k0) + residue
                value = jnp.where(packed_at < start1, v0, v1).astype(BF16)
                send[ch, owner, pl.ds(pl.multiple_of(k0, block), block), :] = value

        recv[ch, me] = send[ch, me]

    def slab(ch, peer, sender):
        return pltpu.make_async_remote_copy(
            src_ref=send.at[ch, peer], dst_ref=recv.at[ch, sender],
            send_sem=send_sem.at[ch, peer], recv_sem=recv_sem.at[ch, sender],
            device_id={"ma": peer}, device_id_type=MESH,
        )

    def extra_slab(peer, sender):
        return pltpu.make_async_remote_copy(
            src_ref=extra_send.at[peer], dst_ref=extra_recv.at[sender],
            send_sem=ex_send.at[peer], recv_sem=ex_recv.at[sender],
            device_id={"ma": peer}, device_id_type=MESH,
        )

    def ship(ch):
        @pl.loop(0, lanes - 1)
        def _(i):
            slab(ch, partner(me, lanes - 1 - i, lanes), me).start()

    pack(0)
    ship(0)
    for ch in range(1, chunks):
        widen(ch)

    tile = lax.broadcasted_iota(jnp.int32, (16, reals), 0)

    @pl.loop(0, lanes)
    def _(owner):
        m0, m1 = m_smem[owner, 0, 0], m_smem[owner, 1, 0]
        start1 = total - m0
        first1 = (m0 + m1 - total - me + lanes - 1) // lanes
        row = jnp.clip(start1 // lanes + first1, 0, rows)
        value = jnp.zeros((16, reals), F32)
        for ch in range(chunks):
            one = wide[ch, pl.ds(row * slots + 2 * owner + 1, 1), :]
            value = jnp.where(tile == ch, one, value)
        extra_send[owner] = value.astype(BF16)

    extra_recv[me] = extra_send[me]

    @pl.loop(0, lanes - 1)
    def _(i):
        extra_slab(partner(me, lanes - 1 - i, lanes), me).start()

    @pl.loop(1, chunks)
    def _(ch):
        pack(ch)
        ship(ch)

    acc_r[...] = jnp.zeros_like(acc_r)
    acc_i[...] = jnp.zeros_like(acc_i)
    my0, my1 = m_smem[me, 0, 0], m_smem[me, 1, 0]
    start1 = total - my0
    end1 = start1 + total - my1
    q = start1 // lanes

    for part in range(2):
        for pol in range(pols):
            pltpu.make_async_copy(
                beam_ref.at[part, pol], beam_buf.at[part, pol], beam_sem.at[part, pol]
            ).wait()

    @pl.loop(1, lanes)
    def _(step):
        peer = partner(me, step, lanes)
        extra_slab(peer, peer).wait_recv()
        extra_slab(peer, peer).wait_send()

    @pl.loop(0, chunks)
    def _(ch):
        @pl.loop(1, lanes)
        def _(step):
            peer = partner(me, step, lanes)
            slab(ch, peer, peer).wait_recv()
            slab(ch, peer, peer).wait_send()

        @pl.loop(0, lanes)
        def _(lane):
            stage[lane] = recv[ch, lane].astype(F32)

        @pl.loop(0, lanes)
        def _(residue):
            lane0 = (residue + my0) % lanes
            lane1 = (residue + my0 + my1) % lanes
            spare_all = extra_recv[lane1].astype(F32)
            spare = jnp.sum(jnp.where(tile == ch, spare_all, 0.0), axis=0, keepdims=True)

            @pl.loop(0, rows // block)
            def _(i):
                k0 = pl.multiple_of(i * block, block)
                v0 = stage[lane0, pl.ds(k0, block), :]
                v1 = stage[lane1, pl.ds(k0, block), :]
                k = row_in_block + k0
                at = lanes * k + residue
                v1 = jnp.where(k == q, spare, v1)
                v1 = jnp.where(at < end1, v1, 0.0)
                mixed[pl.ds(residue + lanes * k0, block, stride=lanes), :] = jnp.where(
                    at < start1, v0, v1
                )

        part = ch // pols
        pol = ch % pols
        sign = (1 - 2 * part).astype(F32)

        @pl.loop(0, total // kblock)
        def _(i):
            at = pl.multiple_of(i * kblock, kblock)
            flat = mixed[pl.ds(at, kblock), :].T
            place = lax.broadcasted_iota(jnp.int32, (reals, kblock), 1) + at
            turned[pl.ds(0, reals), :] = jnp.where(place < start1, flat, 0.0).astype(BF16)
            turned[pl.ds(reals, reals), :] = jnp.where(place < start1, 0.0, flat).astype(BF16)
            both = turned[...]
            acc_r[...] += sign * jnp.dot(
                both, beam_buf[part, pol, pl.ds(at, kblock), :], preferred_element_type=F32
            )
            acc_i[...] += jnp.dot(
                both, beam_buf[1 - part, pol, pl.ds(at, kblock), :], preferred_element_type=F32
            )

    vis_ref[0] = acc_r[...].astype(BF16)
    vis_ref[1] = acc_i[...].astype(BF16)


def exchange(sky, beam, m_values):
    lanes = lax.axis_size("ma")
    parts, pols, rows, slots, reals = sky.shape
    total, bases = beam.shape[2], beam.shape[3]
    chunks = parts * pols
    block, kblock = 32, 512
    m_tile = jnp.zeros((8, 128), jnp.int32).at[:2].set(
        jnp.broadcast_to(m_values[:, None], (2, 128))
    )
    flat = sky.reshape(chunks, rows * slots, reals)
    any_space = pl.BlockSpec(memory_space=pl.ANY)
    vmem = pl.BlockSpec(memory_space=pltpu.VMEM)
    dma = pltpu.SemaphoreType.DMA
    return pl.pallas_call(
        functools.partial(exchange_kernel, lanes, rows, slots, block, kblock),
        out_shape=jax.ShapeDtypeStruct((2, 2 * reals, bases), BF16),
        in_specs=[vmem, any_space, any_space],
        out_specs=vmem,
        scratch_shapes=[
            pltpu.VMEM((lanes, 8, 128), jnp.int32),
            pltpu.SMEM((lanes, 8, 128), jnp.int32),
            pltpu.VMEM((chunks, rows * slots, reals), BF16),
            pltpu.VMEM((chunks, (rows + block) * slots, reals), F32),
            pltpu.VMEM((chunks, lanes, rows, reals), BF16),
            pltpu.VMEM((chunks, lanes, rows, reals), BF16),
            pltpu.VMEM((lanes, 16, reals), BF16),
            pltpu.VMEM((lanes, 16, reals), BF16),
            pltpu.VMEM((2, pols, total, bases), BF16),
            pltpu.VMEM((lanes, rows, reals), F32),
            pltpu.VMEM((total, reals), F32),
            pltpu.VMEM((2 * reals, kblock), BF16),
            pltpu.VMEM((2 * reals, bases), F32),
            pltpu.VMEM((2 * reals, bases), F32),
            dma((lanes,)), dma((lanes,)), dma,
            dma((chunks,)), dma((2, pols)),
            dma((chunks, lanes)), dma((chunks, lanes)), dma((lanes,)), dma((lanes,)),
        ],
        compiler_params=pltpu.CompilerParams(
            collective_id=0, has_side_effects=True, vmem_limit_bytes=64_000_000
        ),
    )(m_tile, flat, beam)


def complex_stack(first_part, second_part):
    return jnp.stack([jnp.stack([first_part, -second_part]), jnp.stack([second_part, first_part])])


def shards(sky_coeffs, beam_transfer, svd_basis, kl_basis, m_values, svd_count, kl_index, kl_count):
    svd_owner = svd_basis[0]
    mode_total = svd_owner.shape[2]
    reals = sky_coeffs.shape[-1]
    selected = jax.vmap(lambda basis_one, chosen: jnp.take(basis_one, chosen, axis=1))(
        kl_basis, kl_index
    )
    visibility = exchange(sky_coeffs[0, :, :, :, 0], beam_transfer[0, 0], m_values)
    visibility = visibility.reshape(2, 2, reals, visibility.shape[-1])
    rotated = jnp.stack(
        [jnp.stack([visibility[0], visibility[1]]), jnp.stack([visibility[1], -visibility[0]])]
    )
    coefficients = jnp.einsum(
        "oqsrb,sqjb->osjr", rotated, svd_owner, preferred_element_type=jnp.float32
    )
    mode_mask = jnp.arange(mode_total, dtype=jnp.int32)[None, :] < svd_count[:, None]
    coefficients = jnp.where(mode_mask[None, :, :, None], coefficients, 0.0).astype(jnp.bfloat16)
    keep_mask = jnp.arange(selected.shape[2], dtype=jnp.int32)[None, :] < kl_count[:, None]
    spread = lax.all_to_all(
        coefficients[:, :, None], "freq", split_axis=4, concat_axis=2, tiled=True
    )
    stacked = complex_stack(spread[0], spread[1])
    kl_out = jnp.einsum("oqsfjr,sqifj->soir", stacked, selected, preferred_element_type=jnp.float32)
    kl_out = jnp.where(keep_mask[:, None, :, None], kl_out, 0.0)
    return kl_out.astype(jnp.bfloat16)


def solution(mesh):
    return jax.shard_map(
        shards,
        mesh=mesh,
        in_specs=(
            P("freq", None, None, None, "ma", None, None),
            P("freq", "ma", None, None, None, None),
            P("freq", "ma", None, None, None),
            P("ma", None, None, None, None),
            P("ma"),
            P("ma"),
            P("ma", None),
            P("ma"),
        ),
        out_specs=P("ma", None, None, "freq"),
        check_vma=False,
    )
```

```python
import functools

import jax
import jax.numpy as jnp
from jax import lax
from jax.experimental import pallas as pl
from jax.experimental.pallas import tpu as pltpu
from jax.sharding import PartitionSpec as P

MESH = pl.DeviceIdType.MESH
F32 = jnp.float32
BF16 = jnp.bfloat16


def partner(me, step, size):
    out, bit = 0, 1
    while bit < size:
        a, b = (me // bit) % 2, (step // bit) % 2
        out = out + bit * (a + b - 2 * a * b)
        bit *= 2
    return out


def exchange_kernel(
    lanes, rows, slots, block, kblock,
    m_ref, sky_ref, beam_ref, vis_ref,
    m_all, m_smem, sky_buf, wide, send, recv, extra_send, extra_recv, beam_buf,
    stage, mixed, turned, acc_r, acc_i,
    m_send, m_recv, m_local, sky_sem, beam_sem, send_sem, recv_sem, ex_send, ex_recv,
):
    me = lax.axis_index("ma")
    chunks = sky_ref.shape[0]
    pols = chunks // 2
    total = lanes * rows
    reals = sky_ref.shape[2]

    for ch in range(chunks):
        pltpu.make_async_copy(sky_ref.at[ch], sky_buf.at[ch], sky_sem.at[ch]).start()
    for part in range(2):
        for pol in range(pols):
            pltpu.make_async_copy(
                beam_ref.at[part, pol], beam_buf.at[part, pol], beam_sem.at[part, pol]
            ).start()

    barrier = pltpu.get_barrier_semaphore()

    @pl.loop(1, lanes)
    def _(step):
        pl.semaphore_signal(
            barrier, inc=1, device_id={"ma": partner(me, step, lanes)}, device_id_type=MESH
        )

    pl.semaphore_wait(barrier, lanes - 1)

    def m_copy(step):
        peer = partner(me, step, lanes)
        return pltpu.make_async_remote_copy(
            src_ref=m_ref, dst_ref=m_all.at[me], send_sem=m_send.at[peer],
            recv_sem=m_recv.at[me], device_id={"ma": peer}, device_id_type=MESH,
        )

    def m_arrival(step):
        peer = partner(me, step, lanes)
        return pltpu.make_async_remote_copy(
            src_ref=m_ref, dst_ref=m_all.at[peer], send_sem=m_send.at[peer],
            recv_sem=m_recv.at[peer], device_id={"ma": peer}, device_id_type=MESH,
        )

    @pl.loop(0, lanes - 1)
    def _(i):
        m_copy(lanes - 1 - i).start()

    m_all[me] = m_ref[...]

    def widen(ch):
        pltpu.make_async_copy(sky_ref.at[ch], sky_buf.at[ch], sky_sem.at[ch]).wait()
        piece = 256

        @pl.loop(0, rows * slots // piece)
        def _(i):
            at = pl.multiple_of(i * piece, piece)
            wide[ch, pl.ds(at, piece), :] = sky_buf[ch, pl.ds(at, piece), :].astype(F32)

        wide[ch, pl.ds(rows * slots, block * slots), :] = jnp.zeros((block * slots, reals), F32)

    widen(0)

    @pl.loop(1, lanes)
    def _(step):
        copy = m_arrival(step)
        copy.wait_recv()
        copy.wait_send()

    local = pltpu.make_async_copy(m_all, m_smem, m_local)
    local.start()
    local.wait()

    row_in_block = lax.broadcasted_iota(jnp.int32, (block, reals), 0)

    def pack(ch):
        @pl.loop(0, lanes)
        def _(owner):
            m0, m1 = m_smem[owner, 0, 0], m_smem[owner, 1, 0]
            start1 = total - m0
            excess = m0 + m1 - total
            first0 = (m0 - me + lanes - 1) // lanes
            first1 = (excess - me + lanes - 1) // lanes
            residue = lanes * first0 + me - m0

            @pl.loop(0, rows // block)
            def _(i):
                k0 = i * block
                r0 = jnp.clip(first0 + k0, 0, rows)
                r1 = jnp.clip(first1 + k0, 0, rows)
                v0 = wide[ch, pl.ds(r0 * slots + 2 * owner, block, stride=slots), :]
                v1 = wide[ch, pl.ds(r1 * slots + 2 * owner + 1, block, stride=slots), :]
                packed_at = lanes * (row_in_block + k0) + residue
                value = jnp.where(packed_at < start1, v0, v1).astype(BF16)
                send[ch, owner, pl.ds(pl.multiple_of(k0, block), block), :] = value

        recv[ch, me] = send[ch, me]

    def slab(ch, peer, sender):
        return pltpu.make_async_remote_copy(
            src_ref=send.at[ch, peer], dst_ref=recv.at[ch, sender],
            send_sem=send_sem.at[ch, peer], recv_sem=recv_sem.at[ch, sender],
            device_id={"ma": peer}, device_id_type=MESH,
        )

    def extra_slab(peer, sender):
        return pltpu.make_async_remote_copy(
            src_ref=extra_send.at[peer], dst_ref=extra_recv.at[sender],
            send_sem=ex_send.at[peer], recv_sem=ex_recv.at[sender],
            device_id={"ma": peer}, device_id_type=MESH,
        )

    half = lanes // 2
    quarter = (4 * me) // lanes
    at_end = (quarter == 0) | (quarter == 3)

    def ship_across(ch):
        @pl.loop(0, lanes - half)
        def _(i):
            slab(ch, partner(me, lanes - 1 - i, lanes), me).start()

    def ship(ch):
        @pl.when(jnp.logical_not(at_end))
        def _():
            ship_across(ch)

        @pl.loop(0, half - 1)
        def _(i):
            slab(ch, partner(me, half - 1 - i, lanes), me).start()

    pack(0)
    ship(0)
    for ch in range(1, chunks):
        widen(ch)

    tile = lax.broadcasted_iota(jnp.int32, (16, reals), 0)

    @pl.loop(0, lanes)
    def _(owner):
        m0, m1 = m_smem[owner, 0, 0], m_smem[owner, 1, 0]
        start1 = total - m0
        first1 = (m0 + m1 - total - me + lanes - 1) // lanes
        row = jnp.clip(start1 // lanes + first1, 0, rows)
        value = jnp.zeros((16, reals), F32)
        for ch in range(chunks):
            one = wide[ch, pl.ds(row * slots + 2 * owner + 1, 1), :]
            value = jnp.where(tile == ch, one, value)
        extra_send[owner] = value.astype(BF16)

    extra_recv[me] = extra_send[me]

    @pl.loop(0, lanes - 1)
    def _(i):
        extra_slab(partner(me, lanes - 1 - i, lanes), me).start()

    @pl.loop(1, chunks)
    def _(ch):
        pack(ch)
        ship(ch)

    @pl.when(at_end)
    def _():
        @pl.loop(0, chunks)
        def _(ch):
            ship_across(ch)

    acc_r[...] = jnp.zeros_like(acc_r)
    acc_i[...] = jnp.zeros_like(acc_i)
    my0, my1 = m_smem[me, 0, 0], m_smem[me, 1, 0]
    start1 = total - my0
    end1 = start1 + total - my1
    q = start1 // lanes

    for part in range(2):
        for pol in range(pols):
            pltpu.make_async_copy(
                beam_ref.at[part, pol], beam_buf.at[part, pol], beam_sem.at[part, pol]
            ).wait()

    @pl.loop(1, lanes)
    def _(step):
        peer = partner(me, step, lanes)
        extra_slab(peer, peer).wait_recv()
        extra_slab(peer, peer).wait_send()

    @pl.loop(0, chunks)
    def _(ch):
        @pl.loop(1, lanes)
        def _(step):
            peer = partner(me, step, lanes)
            slab(ch, peer, peer).wait_recv()
            slab(ch, peer, peer).wait_send()

        @pl.loop(0, lanes)
        def _(lane):
            stage[lane] = recv[ch, lane].astype(F32)

        @pl.loop(0, lanes)
        def _(residue):
            lane0 = (residue + my0) % lanes
            lane1 = (residue + my0 + my1) % lanes
            spare_all = extra_recv[lane1].astype(F32)
            spare = jnp.sum(jnp.where(tile == ch, spare_all, 0.0), axis=0, keepdims=True)

            @pl.loop(0, rows // block)
            def _(i):
                k0 = pl.multiple_of(i * block, block)
                v0 = stage[lane0, pl.ds(k0, block), :]
                v1 = stage[lane1, pl.ds(k0, block), :]
                k = row_in_block + k0
                at = lanes * k + residue
                v1 = jnp.where(k == q, spare, v1)
                v1 = jnp.where(at < end1, v1, 0.0)
                mixed[pl.ds(residue + lanes * k0, block, stride=lanes), :] = jnp.where(
                    at < start1, v0, v1
                )

        part = ch // pols
        pol = ch % pols
        sign = (1 - 2 * part).astype(F32)

        @pl.loop(0, total // kblock)
        def _(i):
            at = pl.multiple_of(i * kblock, kblock)
            flat = mixed[pl.ds(at, kblock), :].T
            place = lax.broadcasted_iota(jnp.int32, (reals, kblock), 1) + at
            turned[pl.ds(0, reals), :] = jnp.where(place < start1, flat, 0.0).astype(BF16)
            turned[pl.ds(reals, reals), :] = jnp.where(place < start1, 0.0, flat).astype(BF16)
            both = turned[...]
            acc_r[...] += sign * jnp.dot(
                both, beam_buf[part, pol, pl.ds(at, kblock), :], preferred_element_type=F32
            )
            acc_i[...] += jnp.dot(
                both, beam_buf[1 - part, pol, pl.ds(at, kblock), :], preferred_element_type=F32
            )

    vis_ref[0] = acc_r[...].astype(BF16)
    vis_ref[1] = acc_i[...].astype(BF16)


def exchange(sky, beam, m_values):
    lanes = lax.axis_size("ma")
    parts, pols, rows, slots, reals = sky.shape
    total, bases = beam.shape[2], beam.shape[3]
    chunks = parts * pols
    block, kblock = 32, 512
    m_tile = jnp.broadcast_to(jnp.tile(m_values, 4)[:, None], (8, 128))
    flat = sky.reshape(chunks, rows * slots, reals)
    any_space = pl.BlockSpec(memory_space=pl.ANY)
    vmem = pl.BlockSpec(memory_space=pltpu.VMEM)
    dma = pltpu.SemaphoreType.DMA
    return pl.pallas_call(
        functools.partial(exchange_kernel, lanes, rows, slots, block, kblock),
        out_shape=jax.ShapeDtypeStruct((2, 2 * reals, bases), BF16),
        in_specs=[vmem, any_space, any_space],
        out_specs=vmem,
        scratch_shapes=[
            pltpu.VMEM((lanes, 8, 128), jnp.int32),
            pltpu.SMEM((lanes, 8, 128), jnp.int32),
            pltpu.VMEM((chunks, rows * slots, reals), BF16),
            pltpu.VMEM((chunks, (rows + block) * slots, reals), F32),
            pltpu.VMEM((chunks, lanes, rows, reals), BF16),
            pltpu.VMEM((chunks, lanes, rows, reals), BF16),
            pltpu.VMEM((lanes, 16, reals), BF16),
            pltpu.VMEM((lanes, 16, reals), BF16),
            pltpu.VMEM((2, pols, total, bases), BF16),
            pltpu.VMEM((lanes, rows, reals), F32),
            pltpu.VMEM((total, reals), F32),
            pltpu.VMEM((2 * reals, kblock), BF16),
            pltpu.VMEM((2 * reals, bases), F32),
            pltpu.VMEM((2 * reals, bases), F32),
            dma((lanes,)), dma((lanes,)), dma,
            dma((chunks,)), dma((2, pols)),
            dma((chunks, lanes)), dma((chunks, lanes)), dma((lanes,)), dma((lanes,)),
        ],
        compiler_params=pltpu.CompilerParams(
            collective_id=0, has_side_effects=True, vmem_limit_bytes=64_000_000
        ),
    )(m_tile, flat, beam)


def complex_stack(first_part, second_part):
    return jnp.stack([jnp.stack([first_part, -second_part]), jnp.stack([second_part, first_part])])


def shards(sky_coeffs, beam_transfer, svd_basis, kl_basis, m_values, svd_count, kl_index, kl_count):
    svd_owner = svd_basis[0]
    mode_total = svd_owner.shape[2]
    reals = sky_coeffs.shape[-1]
    selected = jax.vmap(lambda basis_one, chosen: jnp.take(basis_one, chosen, axis=1))(
        kl_basis, kl_index
    )
    visibility = exchange(sky_coeffs[0, :, :, :, 0], beam_transfer[0, 0], m_values)
    visibility = visibility.reshape(2, 2, reals, visibility.shape[-1])
    rotated = jnp.stack(
        [jnp.stack([visibility[0], visibility[1]]), jnp.stack([visibility[1], -visibility[0]])]
    )
    coefficients = jnp.einsum(
        "oqsrb,sqjb->osjr", rotated, svd_owner, preferred_element_type=jnp.float32
    )
    mode_mask = jnp.arange(mode_total, dtype=jnp.int32)[None, :] < svd_count[:, None]
    coefficients = jnp.where(mode_mask[None, :, :, None], coefficients, 0.0).astype(jnp.bfloat16)
    keep_mask = jnp.arange(selected.shape[2], dtype=jnp.int32)[None, :] < kl_count[:, None]
    spread = lax.all_to_all(
        coefficients[:, :, None], "freq", split_axis=4, concat_axis=2, tiled=True
    )
    stacked = complex_stack(spread[0], spread[1])
    kl_out = jnp.einsum("oqsfjr,sqifj->soir", stacked, selected, preferred_element_type=jnp.float32)
    kl_out = jnp.where(keep_mask[:, None, :, None], kl_out, 0.0)
    return kl_out.astype(jnp.bfloat16)


def solution(mesh):
    return jax.shard_map(
        shards,
        mesh=mesh,
        in_specs=(
            P("freq", None, None, None, "ma", None, None),
            P("freq", "ma", None, None, None, None),
            P("freq", "ma", None, None, None),
            P("ma", None, None, None, None),
            P("ma"),
            P("ma"),
            P("ma", None),
            P("ma"),
        ),
        out_specs=P("ma", None, None, "freq"),
        check_vma=False,
    )
```

```python
import functools

import jax
import jax.numpy as jnp
from jax import lax
from jax.experimental import pallas as pl
from jax.experimental.pallas import tpu as pltpu
from jax.sharding import PartitionSpec as P

MESH = pl.DeviceIdType.MESH
F32 = jnp.float32
BF16 = jnp.bfloat16


def partner(me, step, size):
    out, bit = 0, 1
    while bit < size:
        a, b = (me // bit) % 2, (step // bit) % 2
        out = out + bit * (a + b - 2 * a * b)
        bit *= 2
    return out


def exchange_kernel(
    lanes, rows, slots, block, kblock,
    m_ref, svd_count, kl_count, index_ref, sky_ref, beam_ref, svd_ref, kl_ref, out_ref,
    m_all, m_smem, sky_buf, wide, send, recv, extra_send, extra_recv, beam_buf,
    stage, mixed, turned, acc_r, acc_i,
    svd_buf, kl_buf, chosen, coef_send, coef_recv,
    m_send, m_recv, m_local, sky_sem, beam_sem, send_sem, recv_sem, ex_send, ex_recv,
    basis_sem, coef_sem, coef_arrived,
):
    me = lax.axis_index("ma")
    chunks = sky_ref.shape[0]
    pols = chunks // 2
    total = lanes * rows
    reals = sky_ref.shape[2]

    for ch in range(chunks):
        pltpu.make_async_copy(sky_ref.at[ch], sky_buf.at[ch], sky_sem.at[ch]).start()
    for part in range(2):
        for pol in range(pols):
            pltpu.make_async_copy(
                beam_ref.at[part, pol], beam_buf.at[part, pol], beam_sem.at[part, pol]
            ).start()

    svd_load = pltpu.make_async_copy(svd_ref, svd_buf, basis_sem.at[0])
    kl_load = pltpu.make_async_copy(kl_ref, kl_buf, basis_sem.at[1])
    svd_load.start()
    kl_load.start()
    mine = lax.axis_index("freq")
    bands = coef_send.shape[0]
    share = coef_send.shape[3]

    barrier = pltpu.get_barrier_semaphore()

    @pl.loop(1, lanes)
    def _(step):
        pl.semaphore_signal(
            barrier, inc=1, device_id={"ma": partner(me, step, lanes)}, device_id_type=MESH
        )

    @pl.loop(1, bands)
    def _(step):
        pl.semaphore_signal(
            barrier, inc=1, device_id={"freq": partner(mine, step, bands)}, device_id_type=MESH
        )

    pl.semaphore_wait(barrier, lanes - 1 + bands - 1)

    def m_copy(step):
        peer = partner(me, step, lanes)
        return pltpu.make_async_remote_copy(
            src_ref=m_ref, dst_ref=m_all.at[me], send_sem=m_send.at[peer],
            recv_sem=m_recv.at[me], device_id={"ma": peer}, device_id_type=MESH,
        )

    def m_arrival(step):
        peer = partner(me, step, lanes)
        return pltpu.make_async_remote_copy(
            src_ref=m_ref, dst_ref=m_all.at[peer], send_sem=m_send.at[peer],
            recv_sem=m_recv.at[peer], device_id={"ma": peer}, device_id_type=MESH,
        )

    @pl.loop(0, lanes - 1)
    def _(i):
        m_copy(lanes - 1 - i).start()

    m_all[me] = m_ref[...]

    def widen(ch):
        pltpu.make_async_copy(sky_ref.at[ch], sky_buf.at[ch], sky_sem.at[ch]).wait()
        piece = 256

        @pl.loop(0, rows * slots // piece)
        def _(i):
            at = pl.multiple_of(i * piece, piece)
            wide[ch, pl.ds(at, piece), :] = sky_buf[ch, pl.ds(at, piece), :].astype(F32)

        wide[ch, pl.ds(rows * slots, block * slots), :] = jnp.zeros((block * slots, reals), F32)

    widen(0)

    @pl.loop(1, lanes)
    def _(step):
        copy = m_arrival(step)
        copy.wait_recv()
        copy.wait_send()

    local = pltpu.make_async_copy(m_all, m_smem, m_local)
    local.start()
    local.wait()

    row_in_block = lax.broadcasted_iota(jnp.int32, (block, reals), 0)

    def pack(ch):
        @pl.loop(0, lanes)
        def _(owner):
            m0, m1 = m_smem[owner, 0, 0], m_smem[owner, 1, 0]
            start1 = total - m0
            excess = m0 + m1 - total
            first0 = (m0 - me + lanes - 1) // lanes
            first1 = (excess - me + lanes - 1) // lanes
            residue = lanes * first0 + me - m0

            @pl.loop(0, rows // block)
            def _(i):
                k0 = i * block
                r0 = jnp.clip(first0 + k0, 0, rows)
                r1 = jnp.clip(first1 + k0, 0, rows)
                v0 = wide[ch, pl.ds(r0 * slots + 2 * owner, block, stride=slots), :]
                v1 = wide[ch, pl.ds(r1 * slots + 2 * owner + 1, block, stride=slots), :]
                packed_at = lanes * (row_in_block + k0) + residue
                value = jnp.where(packed_at < start1, v0, v1).astype(BF16)
                send[ch, owner, pl.ds(pl.multiple_of(k0, block), block), :] = value

        recv[ch, me] = send[ch, me]

    def slab(ch, peer, sender):
        return pltpu.make_async_remote_copy(
            src_ref=send.at[ch, peer], dst_ref=recv.at[ch, sender],
            send_sem=send_sem.at[ch, peer], recv_sem=recv_sem.at[ch, sender],
            device_id={"ma": peer}, device_id_type=MESH,
        )

    def extra_slab(peer, sender):
        return pltpu.make_async_remote_copy(
            src_ref=extra_send.at[peer], dst_ref=extra_recv.at[sender],
            send_sem=ex_send.at[peer], recv_sem=ex_recv.at[sender],
            device_id={"ma": peer}, device_id_type=MESH,
        )

    def ship(ch):
        @pl.loop(0, lanes - 1)
        def _(i):
            slab(ch, partner(me, lanes - 1 - i, lanes), me).start()

    pack(0)
    ship(0)
    for ch in range(1, chunks):
        widen(ch)

    tile = lax.broadcasted_iota(jnp.int32, (16, reals), 0)

    @pl.loop(0, lanes)
    def _(owner):
        m0, m1 = m_smem[owner, 0, 0], m_smem[owner, 1, 0]
        start1 = total - m0
        first1 = (m0 + m1 - total - me + lanes - 1) // lanes
        row = jnp.clip(start1 // lanes + first1, 0, rows)
        value = jnp.zeros((16, reals), F32)
        for ch in range(chunks):
            one = wide[ch, pl.ds(row * slots + 2 * owner + 1, 1), :]
            value = jnp.where(tile == ch, one, value)
        extra_send[owner] = value.astype(BF16)

    extra_recv[me] = extra_send[me]

    @pl.loop(0, lanes - 1)
    def _(i):
        extra_slab(partner(me, lanes - 1 - i, lanes), me).start()

    @pl.loop(1, chunks)
    def _(ch):
        pack(ch)
        ship(ch)

    svd_load.wait()
    kl_load.wait()
    modes, kept = kl_buf.shape[2], index_ref.shape[1]
    for slot in range(2):
        column = lax.broadcasted_iota(jnp.int32, (modes, kept), 0)
        place = lax.broadcasted_iota(jnp.int32, (modes, kept), 1)
        hit = (column == index_ref[pl.ds(slot, 1), :]) & (place < kl_count[slot])
        pick = jnp.where(hit, 1.0, 0.0).astype(F32).T.astype(BF16)
        for part in range(2):
            for band in range(bands):
                chosen[slot, part, band] = jnp.dot(
                    pick, kl_buf[slot, part, :, band, :], preferred_element_type=F32
                ).astype(BF16)

    acc_r[...] = jnp.zeros_like(acc_r)
    acc_i[...] = jnp.zeros_like(acc_i)
    my0, my1 = m_smem[me, 0, 0], m_smem[me, 1, 0]
    start1 = total - my0
    end1 = start1 + total - my1
    q = start1 // lanes

    for part in range(2):
        for pol in range(pols):
            pltpu.make_async_copy(
                beam_ref.at[part, pol], beam_buf.at[part, pol], beam_sem.at[part, pol]
            ).wait()

    @pl.loop(1, lanes)
    def _(step):
        peer = partner(me, step, lanes)
        extra_slab(peer, peer).wait_recv()
        extra_slab(peer, peer).wait_send()

    @pl.loop(0, chunks)
    def _(ch):
        @pl.loop(1, lanes)
        def _(step):
            peer = partner(me, step, lanes)
            slab(ch, peer, peer).wait_recv()
            slab(ch, peer, peer).wait_send()

        @pl.loop(0, lanes)
        def _(lane):
            stage[lane] = recv[ch, lane].astype(F32)

        @pl.loop(0, lanes)
        def _(residue):
            lane0 = (residue + my0) % lanes
            lane1 = (residue + my0 + my1) % lanes
            spare_all = extra_recv[lane1].astype(F32)
            spare = jnp.sum(jnp.where(tile == ch, spare_all, 0.0), axis=0, keepdims=True)

            @pl.loop(0, rows // block)
            def _(i):
                k0 = pl.multiple_of(i * block, block)
                v0 = stage[lane0, pl.ds(k0, block), :]
                v1 = stage[lane1, pl.ds(k0, block), :]
                k = row_in_block + k0
                at = lanes * k + residue
                v1 = jnp.where(k == q, spare, v1)
                v1 = jnp.where(at < end1, v1, 0.0)
                mixed[pl.ds(residue + lanes * k0, block, stride=lanes), :] = jnp.where(
                    at < start1, v0, v1
                )

        part = ch // pols
        pol = ch % pols
        sign = (1 - 2 * part).astype(F32)

        @pl.loop(0, total // kblock)
        def _(i):
            at = pl.multiple_of(i * kblock, kblock)
            flat = mixed[pl.ds(at, kblock), :].T
            place = lax.broadcasted_iota(jnp.int32, (reals, kblock), 1) + at
            turned[pl.ds(0, reals), :] = jnp.where(place < start1, flat, 0.0).astype(BF16)
            turned[pl.ds(reals, reals), :] = jnp.where(place < start1, 0.0, flat).astype(BF16)
            both = turned[...]
            acc_r[...] += sign * jnp.dot(
                both, beam_buf[part, pol, pl.ds(at, kblock), :], preferred_element_type=F32
            )
            acc_i[...] += jnp.dot(
                both, beam_buf[1 - part, pol, pl.ds(at, kblock), :], preferred_element_type=F32
            )

    def nt(left, right):
        return lax.dot_general(left, right, (((1,), (1,)), ((), ())), preferred_element_type=F32)

    modes_all = svd_buf.shape[2]
    for slot in range(2):
        vr = acc_r[pl.ds(slot * reals, reals), :].astype(BF16)
        vi = acc_i[pl.ds(slot * reals, reals), :].astype(BF16)
        ur, ui = svd_buf[slot, 0], svd_buf[slot, 1]
        keep = lax.broadcasted_iota(jnp.int32, (reals, modes_all), 1) < svd_count[slot]
        real = jnp.where(keep, nt(vr, ur) + nt(vi, ui), 0.0).astype(BF16)
        imag = jnp.where(keep, nt(vi, ur) - nt(vr, ui), 0.0).astype(BF16)
        for band in range(bands):
            coef_send[band, 0, slot] = real[band * share:(band + 1) * share]
            coef_send[band, 1, slot] = imag[band * share:(band + 1) * share]

    def coef_copy(peer, sender):
        return pltpu.make_async_remote_copy(
            src_ref=coef_send.at[peer], dst_ref=coef_recv.at[sender],
            send_sem=coef_sem.at[peer], recv_sem=coef_arrived.at[sender],
            device_id={"freq": peer}, device_id_type=MESH,
        )

    @pl.loop(0, bands - 1)
    def _(i):
        coef_copy(partner(mine, bands - 1 - i, bands), mine).start()

    coef_recv[mine] = coef_send[mine]

    @pl.loop(1, bands)
    def _(step):
        peer = partner(mine, step, bands)
        coef_copy(peer, peer).wait_recv()
        coef_copy(peer, peer).wait_send()

    for slot in range(2):
        real = jnp.zeros((kept, share), F32)
        imag = jnp.zeros((kept, share), F32)
        for band in range(bands):
            kr, ki = chosen[slot, 0, band], chosen[slot, 1, band]
            sr, si = coef_recv[band, 0, slot], coef_recv[band, 1, slot]
            real = real + nt(kr, sr) - nt(ki, si)
            imag = imag + nt(kr, si) + nt(ki, sr)
        out_ref[slot, 0] = real.astype(BF16)
        out_ref[slot, 1] = imag.astype(BF16)


def exchange(sky, beam, svd, kl, m_values, svd_count, kl_index, kl_count):
    lanes, bands = lax.axis_size("ma"), lax.axis_size("freq")
    kept, share = kl_index.shape[1], sky.shape[-1] // bands
    parts, pols, rows, slots, reals = sky.shape
    total, bases = beam.shape[2], beam.shape[3]
    chunks = parts * pols
    block, kblock = 32, 512
    m_tile = jnp.broadcast_to(jnp.tile(m_values, 4)[:, None], (8, 128))
    flat = sky.reshape(chunks, rows * slots, reals)
    any_space = pl.BlockSpec(memory_space=pl.ANY)
    vmem = pl.BlockSpec(memory_space=pltpu.VMEM)
    smem = pl.BlockSpec(memory_space=pltpu.SMEM)
    dma = pltpu.SemaphoreType.DMA
    return pl.pallas_call(
        functools.partial(exchange_kernel, lanes, rows, slots, block, kblock),
        out_shape=jax.ShapeDtypeStruct((2, 2, kept, share), BF16),
        in_specs=[vmem, smem, smem, vmem, any_space, any_space, any_space, any_space],
        out_specs=vmem,
        scratch_shapes=[
            pltpu.VMEM((lanes, 8, 128), jnp.int32),
            pltpu.SMEM((lanes, 8, 128), jnp.int32),
            pltpu.VMEM((chunks, rows * slots, reals), BF16),
            pltpu.VMEM((chunks, (rows + block) * slots, reals), F32),
            pltpu.VMEM((chunks, lanes, rows, reals), BF16),
            pltpu.VMEM((chunks, lanes, rows, reals), BF16),
            pltpu.VMEM((lanes, 16, reals), BF16),
            pltpu.VMEM((lanes, 16, reals), BF16),
            pltpu.VMEM((2, pols, total, bases), BF16),
            pltpu.VMEM((lanes, rows, reals), F32),
            pltpu.VMEM((total, reals), F32),
            pltpu.VMEM((2 * reals, kblock), BF16),
            pltpu.VMEM((2 * reals, bases), F32),
            pltpu.VMEM((2 * reals, bases), F32),
            pltpu.VMEM(svd.shape, BF16),
            pltpu.VMEM(kl.shape, BF16),
            pltpu.VMEM((2, 2, bands, kept, svd.shape[2]), BF16),
            pltpu.VMEM((bands, 2, 2, share, svd.shape[2]), BF16),
            pltpu.VMEM((bands, 2, 2, share, svd.shape[2]), BF16),
            dma((lanes,)), dma((lanes,)), dma,
            dma((chunks,)), dma((2, pols)),
            dma((chunks, lanes)), dma((chunks, lanes)), dma((lanes,)), dma((lanes,)),
            dma((2,)), dma((bands,)), dma((bands,)),
        ],
        compiler_params=pltpu.CompilerParams(
            collective_id=0, has_side_effects=True, vmem_limit_bytes=64_000_000
        ),
    )(m_tile, svd_count, kl_count, kl_index, flat, beam, svd, kl)


def shards(sky_coeffs, beam_transfer, svd_basis, kl_basis, m_values, svd_count, kl_index, kl_count):
    return exchange(
        sky_coeffs[0, :, :, :, 0], beam_transfer[0, 0], svd_basis[0], kl_basis,
        m_values, svd_count, kl_index, kl_count,
    )


def solution(mesh):
    return jax.shard_map(
        shards,
        mesh=mesh,
        in_specs=(
            P("freq", None, None, None, "ma", None, None),
            P("freq", "ma", None, None, None, None),
            P("freq", "ma", None, None, None),
            P("ma", None, None, None, None),
            P("ma"),
            P("ma"),
            P("ma", None),
            P("ma"),
        ),
        out_specs=P("ma", None, None, "freq"),
        check_vma=False,
    )
```

```python
import functools

import jax
import jax.numpy as jnp
from jax import lax
from jax.experimental import pallas as pl
from jax.experimental.pallas import tpu as pltpu
from jax.sharding import PartitionSpec as P

MESH = pl.DeviceIdType.MESH
F32 = jnp.float32
BF16 = jnp.bfloat16


def partner(me, step, size):
    out, bit = 0, 1
    while bit < size:
        a, b = (me // bit) % 2, (step // bit) % 2
        out = out + bit * (a + b - 2 * a * b)
        bit *= 2
    return out


def exchange_kernel(
    lanes, rows, slots, block, kblock,
    m_ref, svd_count, kl_count, index_ref, sky_ref, beam_ref, svd_ref, kl_ref, out_ref,
    m_all, m_smem, sky_buf, wide, send, recv, extra_send, extra_recv, beam_buf,
    stage, mixed, acc_r, acc_i,
    svd_buf, kl_buf, chosen, coef_send, coef_recv,
    m_send, m_recv, m_local, sky_sem, beam_sem, send_sem, recv_sem, ex_send, ex_recv,
    basis_sem, coef_sem, coef_arrived,
):
    me = lax.axis_index("ma")
    chunks = sky_ref.shape[0]
    pols = chunks // 2
    total = lanes * rows
    reals = sky_ref.shape[2]

    for ch in range(chunks):
        pltpu.make_async_copy(sky_ref.at[ch], sky_buf.at[ch], sky_sem.at[ch]).start()
    for part in range(2):
        for pol in range(pols):
            pltpu.make_async_copy(
                beam_ref.at[part, pol], beam_buf.at[part, pol], beam_sem.at[part, pol]
            ).start()

    svd_load = pltpu.make_async_copy(svd_ref, svd_buf, basis_sem.at[0])
    kl_load = pltpu.make_async_copy(kl_ref, kl_buf, basis_sem.at[1])
    svd_load.start()
    kl_load.start()
    mine = lax.axis_index("freq")
    bands = coef_send.shape[0]
    share = coef_send.shape[3]

    barrier = pltpu.get_barrier_semaphore()

    @pl.loop(1, lanes)
    def _(step):
        pl.semaphore_signal(
            barrier, inc=1, device_id={"ma": partner(me, step, lanes)}, device_id_type=MESH
        )

    @pl.loop(1, bands)
    def _(step):
        pl.semaphore_signal(
            barrier, inc=1, device_id={"freq": partner(mine, step, bands)}, device_id_type=MESH
        )

    pl.semaphore_wait(barrier, lanes - 1 + bands - 1)

    def m_copy(step):
        peer = partner(me, step, lanes)
        return pltpu.make_async_remote_copy(
            src_ref=m_ref, dst_ref=m_all.at[me], send_sem=m_send.at[peer],
            recv_sem=m_recv.at[me], device_id={"ma": peer}, device_id_type=MESH,
        )

    def m_arrival(step):
        peer = partner(me, step, lanes)
        return pltpu.make_async_remote_copy(
            src_ref=m_ref, dst_ref=m_all.at[peer], send_sem=m_send.at[peer],
            recv_sem=m_recv.at[peer], device_id={"ma": peer}, device_id_type=MESH,
        )

    @pl.loop(0, lanes - 1)
    def _(i):
        m_copy(lanes - 1 - i).start()

    m_all[me] = m_ref[...]

    def widen(ch):
        pltpu.make_async_copy(sky_ref.at[ch], sky_buf.at[ch], sky_sem.at[ch]).wait()
        piece = 256

        @pl.loop(0, rows * slots // piece)
        def _(i):
            at = pl.multiple_of(i * piece, piece)
            wide[ch, pl.ds(at, piece), :] = sky_buf[ch, pl.ds(at, piece), :].astype(F32)

        wide[ch, pl.ds(rows * slots, block * slots), :] = jnp.zeros((block * slots, reals), F32)

    widen(0)

    @pl.loop(1, lanes)
    def _(step):
        copy = m_arrival(step)
        copy.wait_recv()
        copy.wait_send()

    local = pltpu.make_async_copy(m_all, m_smem, m_local)
    local.start()
    local.wait()

    row_in_block = lax.broadcasted_iota(jnp.int32, (block, reals), 0)

    def pack(ch):
        @pl.loop(0, lanes)
        def _(owner):
            m0, m1 = m_smem[owner, 0, 0], m_smem[owner, 1, 0]
            start1 = total - m0
            excess = m0 + m1 - total
            first0 = (m0 - me + lanes - 1) // lanes
            first1 = (excess - me + lanes - 1) // lanes
            residue = lanes * first0 + me - m0

            @pl.loop(0, rows // block, unroll=True)
            def _(i):
                k0 = i * block
                r0 = jnp.clip(first0 + k0, 0, rows)
                r1 = jnp.clip(first1 + k0, 0, rows)
                v0 = wide[ch, pl.ds(r0 * slots + 2 * owner, block, stride=slots), :]
                v1 = wide[ch, pl.ds(r1 * slots + 2 * owner + 1, block, stride=slots), :]
                packed_at = lanes * (row_in_block + k0) + residue
                value = jnp.where(packed_at < start1, v0, v1).astype(BF16)
                send[ch, owner, pl.ds(pl.multiple_of(k0, block), block), :] = value

        recv[ch, me] = send[ch, me]

    def slab(ch, peer, sender):
        return pltpu.make_async_remote_copy(
            src_ref=send.at[ch, peer], dst_ref=recv.at[ch, sender],
            send_sem=send_sem.at[ch, peer], recv_sem=recv_sem.at[ch, sender],
            device_id={"ma": peer}, device_id_type=MESH,
        )

    def extra_slab(peer, sender):
        return pltpu.make_async_remote_copy(
            src_ref=extra_send.at[peer], dst_ref=extra_recv.at[sender],
            send_sem=ex_send.at[peer], recv_sem=ex_recv.at[sender],
            device_id={"ma": peer}, device_id_type=MESH,
        )

    def ship(ch):
        @pl.loop(0, lanes - 1)
        def _(i):
            slab(ch, partner(me, lanes - 1 - i, lanes), me).start()

    pack(0)
    ship(0)
    for ch in range(1, chunks):
        widen(ch)

    tile = lax.broadcasted_iota(jnp.int32, (16, reals), 0)

    @pl.loop(0, lanes)
    def _(owner):
        m0, m1 = m_smem[owner, 0, 0], m_smem[owner, 1, 0]
        start1 = total - m0
        first1 = (m0 + m1 - total - me + lanes - 1) // lanes
        row = jnp.clip(start1 // lanes + first1, 0, rows)
        value = jnp.zeros((16, reals), F32)
        for ch in range(chunks):
            one = wide[ch, pl.ds(row * slots + 2 * owner + 1, 1), :]
            value = jnp.where(tile == ch, one, value)
        extra_send[owner] = value.astype(BF16)

    extra_recv[me] = extra_send[me]

    @pl.loop(0, lanes - 1)
    def _(i):
        extra_slab(partner(me, lanes - 1 - i, lanes), me).start()

    @pl.loop(1, chunks)
    def _(ch):
        pack(ch)
        ship(ch)

    svd_load.wait()
    kl_load.wait()
    modes, kept = kl_buf.shape[2], index_ref.shape[1]
    for slot in range(2):
        column = lax.broadcasted_iota(jnp.int32, (modes, kept), 0)
        place = lax.broadcasted_iota(jnp.int32, (modes, kept), 1)
        hit = (column == index_ref[pl.ds(slot, 1), :]) & (place < kl_count[slot])
        pick = jnp.where(hit, 1.0, 0.0).astype(F32).T.astype(BF16)
        for part in range(2):
            for band in range(bands):
                chosen[slot, part, band] = jnp.dot(
                    pick, kl_buf[slot, part, :, band, :], preferred_element_type=F32
                ).astype(BF16)

    acc_r[...] = jnp.zeros_like(acc_r)
    acc_i[...] = jnp.zeros_like(acc_i)
    my0, my1 = m_smem[me, 0, 0], m_smem[me, 1, 0]
    start1 = total - my0
    end1 = start1 + total - my1
    q = start1 // lanes

    for part in range(2):
        for pol in range(pols):
            pltpu.make_async_copy(
                beam_ref.at[part, pol], beam_buf.at[part, pol], beam_sem.at[part, pol]
            ).wait()

    @pl.loop(1, lanes)
    def _(step):
        peer = partner(me, step, lanes)
        extra_slab(peer, peer).wait_recv()
        extra_slab(peer, peer).wait_send()

    @pl.loop(0, chunks)
    def _(ch):
        @pl.loop(1, lanes)
        def _(step):
            peer = partner(me, step, lanes)
            slab(ch, peer, peer).wait_recv()
            slab(ch, peer, peer).wait_send()

        @pl.loop(0, lanes)
        def _(lane):
            stage[lane] = recv[ch, lane].astype(F32)

        @pl.loop(0, lanes)
        def _(residue):
            lane0 = (residue + my0) % lanes
            lane1 = (residue + my0 + my1) % lanes
            spare_all = extra_recv[lane1].astype(F32)
            spare = jnp.sum(jnp.where(tile == ch, spare_all, 0.0), axis=0, keepdims=True)

            @pl.loop(0, rows // block, unroll=True)
            def _(i):
                k0 = pl.multiple_of(i * block, block)
                v0 = stage[lane0, pl.ds(k0, block), :]
                v1 = stage[lane1, pl.ds(k0, block), :]
                k = row_in_block + k0
                at = lanes * k + residue
                v1 = jnp.where(k == q, spare, v1)
                v1 = jnp.where(at < end1, v1, 0.0)
                mixed[pl.ds(residue + lanes * k0, block, stride=lanes), :] = jnp.where(
                    at < start1, v0, v1
                )

        part = ch // pols
        pol = ch % pols
        sign = (1 - 2 * part).astype(F32)

        @pl.loop(0, total // kblock, unroll=True)
        def _(i):
            at = pl.multiple_of(i * kblock, kblock)
            flat = mixed[pl.ds(at, kblock), :].T
            place = lax.broadcasted_iota(jnp.int32, (reals, kblock), 1) + at
            both = jnp.concatenate(
                [jnp.where(place < start1, flat, 0.0), jnp.where(place < start1, 0.0, flat)], axis=0
            ).astype(BF16)
            acc_r[...] += sign * jnp.dot(
                both, beam_buf[part, pol, pl.ds(at, kblock), :], preferred_element_type=F32
            )
            acc_i[...] += jnp.dot(
                both, beam_buf[1 - part, pol, pl.ds(at, kblock), :], preferred_element_type=F32
            )

    def nt(left, right):
        return lax.dot_general(left, right, (((1,), (1,)), ((), ())), preferred_element_type=F32)

    modes_all = svd_buf.shape[2]
    for slot in range(2):
        vr = acc_r[pl.ds(slot * reals, reals), :].astype(BF16)
        vi = acc_i[pl.ds(slot * reals, reals), :].astype(BF16)
        ur, ui = svd_buf[slot, 0], svd_buf[slot, 1]
        keep = lax.broadcasted_iota(jnp.int32, (reals, modes_all), 1) < svd_count[slot]
        real = jnp.where(keep, nt(vr, ur) + nt(vi, ui), 0.0).astype(BF16)
        imag = jnp.where(keep, nt(vi, ur) - nt(vr, ui), 0.0).astype(BF16)
        for band in range(bands):
            coef_send[band, 0, slot] = real[band * share:(band + 1) * share]
            coef_send[band, 1, slot] = imag[band * share:(band + 1) * share]

    def coef_copy(peer, sender):
        return pltpu.make_async_remote_copy(
            src_ref=coef_send.at[peer], dst_ref=coef_recv.at[sender],
            send_sem=coef_sem.at[peer], recv_sem=coef_arrived.at[sender],
            device_id={"freq": peer}, device_id_type=MESH,
        )

    @pl.loop(0, bands - 1)
    def _(i):
        coef_copy(partner(mine, bands - 1 - i, bands), mine).start()

    coef_recv[mine] = coef_send[mine]

    @pl.loop(1, bands)
    def _(step):
        peer = partner(mine, step, bands)
        coef_copy(peer, peer).wait_recv()
        coef_copy(peer, peer).wait_send()

    for slot in range(2):
        real = jnp.zeros((kept, share), F32)
        imag = jnp.zeros((kept, share), F32)
        for band in range(bands):
            kr, ki = chosen[slot, 0, band], chosen[slot, 1, band]
            sr, si = coef_recv[band, 0, slot], coef_recv[band, 1, slot]
            real = real + nt(kr, sr) - nt(ki, si)
            imag = imag + nt(kr, si) + nt(ki, sr)
        out_ref[slot, 0] = real.astype(BF16)
        out_ref[slot, 1] = imag.astype(BF16)


def exchange(sky, beam, svd, kl, m_values, svd_count, kl_index, kl_count):
    lanes, bands = lax.axis_size("ma"), lax.axis_size("freq")
    kept, share = kl_index.shape[1], sky.shape[-1] // bands
    parts, pols, rows, slots, reals = sky.shape
    total, bases = beam.shape[2], beam.shape[3]
    chunks = parts * pols
    block, kblock = 32, 512
    m_tile = jnp.broadcast_to(jnp.tile(m_values, 4)[:, None], (8, 128))
    flat = sky.reshape(chunks, rows * slots, reals)
    any_space = pl.BlockSpec(memory_space=pl.ANY)
    vmem = pl.BlockSpec(memory_space=pltpu.VMEM)
    smem = pl.BlockSpec(memory_space=pltpu.SMEM)
    dma = pltpu.SemaphoreType.DMA
    return pl.pallas_call(
        functools.partial(exchange_kernel, lanes, rows, slots, block, kblock),
        out_shape=jax.ShapeDtypeStruct((2, 2, kept, share), BF16),
        in_specs=[vmem, smem, smem, vmem, any_space, any_space, any_space, any_space],
        out_specs=vmem,
        scratch_shapes=[
            pltpu.VMEM((lanes, 8, 128), jnp.int32),
            pltpu.SMEM((lanes, 8, 128), jnp.int32),
            pltpu.VMEM((chunks, rows * slots, reals), BF16),
            pltpu.VMEM((chunks, (rows + block) * slots, reals), F32),
            pltpu.VMEM((chunks, lanes, rows, reals), BF16),
            pltpu.VMEM((chunks, lanes, rows, reals), BF16),
            pltpu.VMEM((lanes, 16, reals), BF16),
            pltpu.VMEM((lanes, 16, reals), BF16),
            pltpu.VMEM((2, pols, total, bases), BF16),
            pltpu.VMEM((lanes, rows, reals), F32),
            pltpu.VMEM((total, reals), F32),
            pltpu.VMEM((2 * reals, bases), F32),
            pltpu.VMEM((2 * reals, bases), F32),
            pltpu.VMEM(svd.shape, BF16),
            pltpu.VMEM(kl.shape, BF16),
            pltpu.VMEM((2, 2, bands, kept, svd.shape[2]), BF16),
            pltpu.VMEM((bands, 2, 2, share, svd.shape[2]), BF16),
            pltpu.VMEM((bands, 2, 2, share, svd.shape[2]), BF16),
            dma((lanes,)), dma((lanes,)), dma,
            dma((chunks,)), dma((2, pols)),
            dma((chunks, lanes)), dma((chunks, lanes)), dma((lanes,)), dma((lanes,)),
            dma((2,)), dma((bands,)), dma((bands,)),
        ],
        compiler_params=pltpu.CompilerParams(
            collective_id=0, has_side_effects=True, vmem_limit_bytes=64_000_000
        ),
    )(m_tile, svd_count, kl_count, kl_index, flat, beam, svd, kl)


def shards(sky_coeffs, beam_transfer, svd_basis, kl_basis, m_values, svd_count, kl_index, kl_count):
    return exchange(
        sky_coeffs[0, :, :, :, 0], beam_transfer[0, 0], svd_basis[0], kl_basis,
        m_values, svd_count, kl_index, kl_count,
    )


def solution(mesh):
    return jax.shard_map(
        shards,
        mesh=mesh,
        in_specs=(
            P("freq", None, None, None, "ma", None, None),
            P("freq", "ma", None, None, None, None),
            P("freq", "ma", None, None, None),
            P("ma", None, None, None, None),
            P("ma"),
            P("ma"),
            P("ma", None),
            P("ma"),
        ),
        out_specs=P("ma", None, None, "freq"),
        check_vma=False,
    )
```
